256 devices in a mesh: ctx: 64 (over z, y, core), head: 4 (over x).
Axes of the slice: x: 4, y: 4, z: 8, core: 2. Of those that a mesh axis runs over, the one named last changes fastest.
Arguments:
- queries: bfloat16 [32768, 32, 128], P(('ctx', 'head')), may hold values from -1.796875 to 1.796875
- key_vectors: bfloat16 [32768, 32, 128], P(('ctx', 'head')), may hold values from -1.796875 to 1.796875
- value_vectors: bfloat16 [32768, 32, 128], P(('ctx', 'head')), may hold values from -9.9 to 9.9
- output_grad: bfloat16 [32768, 32, 128], P(('ctx', 'head')), may hold values from -9.9 to 9.9
- decay_rate: float32 [32], replicated, may hold values from 0 to 1, as said below
- norm_gain: float32 [32, 128], replicated, may hold values from 0.25 to 1.75
Outputs:
- normed: bfloat16 [32768, 32, 128], P(('ctx', 'head'))
- query_gradient: bfloat16 [32768, 32, 128], P(('ctx', 'head'))
- grad_keys: bfloat16 [32768, 32, 128], P(('ctx', 'head'))
- value_gradient: bfloat16 [32768, 32, 128], P(('ctx', 'head'))
The draws below stay inside these ranges and needn't reach their ends.
Inputs may be any that keep to these rules, and one draw needn't show every extreme that they name: `decay_rate`: each head's rate is positive; a head's state is multiplied by exp(-rate) at every position.
All inputs are finite; a program needn't handle non-finite values.
Results may differ from the reference program's by a relative error of at most 0.012.
Values may be sent and summed in bfloat16 or wider, within the bound.
A program may use at most 128 MiB of HBM per device.

```python
import math
import jax
import jax.numpy as jnp
from jax import lax

HD = 128
HEADS = 32
STRETCH = 128
TOKENS = 32768
N_CTX = 64
N_HEAD = 4


def draw_decay_rate(key, part):
    pick_key = jax.random.fold_in(key, 11)
    fast_key = jax.random.fold_in(key, 12)
    slow_key = jax.random.fold_in(key, 13)
    middle_key = jax.random.fold_in(key, 14)
    ordering = jax.random.permutation(pick_key, HEADS)
    fast_count = HEADS // 4
    middle_count = HEADS // 4
    is_fast = ordering < fast_count
    is_middle = jnp.logical_and(ordering >= fast_count, ordering < fast_count + middle_count)
    fast_rate = jnp.exp(jax.random.uniform(fast_key, (HEADS,), jnp.float32, math.log(1.0 / 50.0), math.log(1.0 / 30.0)))
    middle_rate = jnp.exp(jax.random.uniform(middle_key, (HEADS,), jnp.float32, math.log(1.0 / 2000.0), math.log(1.0 / 300.0)))
    slow_rate = jnp.exp(jax.random.uniform(slow_key, (HEADS,), jnp.float32, math.log(0.1), 0.0)) * (math.log(10.0) / TOKENS)
    return jnp.where(is_fast, fast_rate, jnp.where(is_middle, middle_rate, slow_rate)).astype(jnp.float32)


def stretch_levels(key):
    level_key = jax.random.fold_in(key, 21)
    exponent = jax.random.uniform(level_key, (TOKENS // STRETCH, 1, HEADS, 1), jnp.float32, -7.0, 0.5)
    return jnp.exp(exponent)


def leveled_draw(key, salt):
    entry_key = jax.random.fold_in(key, salt)
    shape = (TOKENS // STRETCH, STRETCH, HEADS, HD)
    base = jnp.clip(jax.random.normal(entry_key, shape, jnp.float32), -6.0, 6.0)
    return (base * stretch_levels(key)).reshape(TOKENS, HEADS, HD).astype(jnp.bfloat16)


def draw_value_vectors(key, part):
    return leveled_draw(key, 22)


def draw_output_grad(key, part):
    return leveled_draw(key, 23)


def shard_levels(key, shape, split, smallest, largest):
    def one(axis_at, shards_of):
        heights = jax.random.uniform(jax.random.fold_in(jax.random.fold_in(key, 6), axis_at), (shards_of,), jnp.float32, smallest / len(split), largest / len(split))
        return jnp.repeat(jnp.exp(heights), shape[axis_at] // shards_of).reshape((-1,) + (1,) * (len(shape) - axis_at - 1))

    gain = one(*split[0])
    for cut in split[1:]:
        gain = gain * one(*cut)
    return gain


def centred(own_key, dims, scale, reach, pieces=(), dtype=jnp.bfloat16):
    drawn = scale * jax.random.normal(own_key, dims, jnp.float32)
    if pieces:
        drawn = drawn * shard_levels(own_key, dims, pieces, -0.22, 0.18)
    return jnp.clip(drawn, -reach, reach).astype(dtype)


def setup_inputs(seed: int = 0) -> dict:
    keys = jax.random.split(jax.random.key(seed), 7)
    queries = centred(keys[0], (TOKENS, HEADS, HD), 0.3, 1.796875, ((0, 256),))
    key_vectors = centred(keys[1], (TOKENS, HEADS, HD), 0.3, 1.796875, ((0, 256),))
    value_vectors = draw_value_vectors(jax.random.fold_in(keys[6], 71), 0)
    output_grad = draw_output_grad(jax.random.fold_in(keys[6], 71), 0)
    decay_rate = draw_decay_rate(jax.random.fold_in(keys[6], 71), 0)
    norm_gain = jnp.clip(1.0 + 0.15 * jax.random.normal(keys[5], (HEADS, HD), jnp.float32), 0.25, 1.75)
    return {"queries": queries, "key_vectors": key_vectors, "value_vectors": value_vectors, "output_grad": output_grad, "decay_rate": decay_rate, "norm_gain": norm_gain}


def carry_stretches(stretch_states, decay_value, length, forward):
    stretch_order = jnp.arange(N_HEAD).astype(jnp.float32)
    place_in = stretch_order if forward else N_HEAD - 1.0 - stretch_order
    states_float = stretch_states.astype(jnp.float32)
    fold_weights = jnp.exp(-decay_value * length * (N_HEAD - 1.0 - place_in))
    block_state = jnp.einsum('k,bkde->bde', fold_weights, states_float, precision=lax.Precision.HIGHEST).astype(jnp.bfloat16).astype(jnp.float32)
    span_decay = jnp.exp(-decay_value * length * N_HEAD)

    def carry_step(state, piece):
        return (span_decay * state + piece, state)
    empty_state = jnp.zeros(block_state.shape[1:], jnp.float32)
    final_state, carried = lax.scan(carry_step, empty_state, block_state, reverse=not forward)
    lead_decay = jnp.exp(-decay_value * length * place_in)
    stretch_gap = place_in[:, None] - 1.0 - place_in[None, :]
    inner_weights = jnp.where(stretch_gap >= 0, jnp.exp(-decay_value * length * jnp.maximum(stretch_gap, 0.0)), 0.0)
    spread = lead_decay[None, :, None, None] * carried[:, None] + jnp.einsum('kq,bqde->bkde', inner_weights, states_float, precision=lax.Precision.HIGHEST)
    return spread.reshape(N_CTX * N_HEAD, HD, HD).astype(jnp.bfloat16).astype(jnp.float32)

def one_head(operands):
    query_blocks, key_blocks, value_blocks, grad_blocks, decay_value, gain_row = operands
    length = query_blocks.shape[1]
    head_size = query_blocks.shape[2]
    steps = jnp.arange(length).astype(jnp.float32)
    offset = steps[:, None] - steps[None, :]
    decay_weight_mask = jnp.where(offset >= 0, jnp.exp(-decay_value * jnp.maximum(offset, 0.0)), 0.0)
    per_head_decay = jnp.exp(-decay_value * (steps + 1.0))[:, None]
    trailing_decay = jnp.exp(-decay_value * (length - 1.0 - steps))[:, None]
    query_widened = query_blocks.astype(jnp.float32)
    key_widened = key_blocks.astype(jnp.float32)
    value_widened = value_blocks.astype(jnp.float32)
    scores = jnp.einsum('nid,njd->nij', query_widened, key_widened)
    attention_matrix = (scores * decay_weight_mask).astype(jnp.bfloat16)
    key_decayed = (key_widened * trailing_decay).astype(jnp.bfloat16)
    local_state = jnp.einsum('njd,nje->nde', key_decayed.astype(jnp.float32), value_widened).astype(jnp.bfloat16)
    incoming_portion = carry_stretches(local_state.reshape(N_CTX, N_HEAD, head_size, head_size), decay_value, length * 1.0, True)
    output_rows = jnp.einsum('ywt,ytg->ywg', attention_matrix.astype(jnp.float32), value_widened)
    output_rows = output_rows + per_head_decay * jnp.einsum('wbr,wrx->wbx', query_widened, incoming_portion)
    inv_rms = lax.rsqrt(lax.optimization_barrier(jnp.mean(output_rows * output_rows, axis=-1, keepdims=True)) + 1e-06)
    unit_rows = output_rows * inv_rms
    normed = (unit_rows * gain_row).astype(jnp.bfloat16)
    scaled = gain_row * grad_blocks.astype(jnp.float32)
    grad_out = (inv_rms * (scaled - unit_rows * lax.optimization_barrier(jnp.mean(scaled * unit_rows, axis=-1, keepdims=True)))).astype(jnp.bfloat16)
    gradient_widened = grad_out.astype(jnp.float32)
    query_with_decay = (query_widened * per_head_decay).astype(jnp.bfloat16)
    state_gradient = jnp.einsum('lou,loz->luz', query_with_decay.astype(jnp.float32), gradient_widened).astype(jnp.bfloat16)
    later_portion = carry_stretches(state_gradient.reshape(N_CTX, N_HEAD, head_size, head_size), decay_value, length * 1.0, False)
    score_gradient = (jnp.einsum('vuy,vsy->vus', gradient_widened, value_widened) * decay_weight_mask).astype(jnp.bfloat16).astype(jnp.float32)
    query_gradient = jnp.einsum('zwc,zca->zwa', score_gradient, key_widened) + per_head_decay * jnp.einsum('rcq,rwq->rcw', gradient_widened, incoming_portion)
    grad_keys = jnp.einsum('nij,nid->njd', score_gradient, query_widened) + trailing_decay * jnp.einsum('nje,nde->njd', value_widened, later_portion)
    value_gradient = jnp.einsum('qml,qmb->qlb', attention_matrix.astype(jnp.float32), gradient_widened) + trailing_decay * jnp.einsum('opv,ovr->opr', key_widened, later_portion)
    return (normed, query_gradient.astype(jnp.bfloat16), grad_keys.astype(jnp.bfloat16), value_gradient.astype(jnp.bfloat16))

def reference(queries, key_vectors, value_vectors, output_grad, decay_rate, norm_gain):

    def to_heads(array):
        return array.reshape(N_CTX * N_HEAD, STRETCH, HEADS, HD).transpose(2, 0, 1, 3)

    def to_tokens(array):
        return array.transpose(1, 2, 0, 3).reshape(TOKENS, HEADS, HD)
    results = lax.map(one_head, (to_heads(queries), to_heads(key_vectors), to_heads(value_vectors), to_heads(output_grad), decay_rate.astype(jnp.float32), norm_gain.astype(jnp.float32)))
    return (to_tokens(results[0]), to_tokens(results[1]), to_tokens(results[2]), to_tokens(results[3]))
```

```python
import functools

import jax
import jax.numpy as jnp
from jax import lax
from jax.experimental import pallas as pl
from jax.experimental.pallas import tpu as pltpu
from jax.sharding import PartitionSpec as P

MESH = pl.DeviceIdType.MESH
NZ, NY, NCORE, NX = 8, 4, 2, 4
ROW = NCORE * NX
PER = 4
F32 = jnp.float32
BF16 = jnp.bfloat16


def dot(a, b, ca, cb):
    return lax.dot_general(a, b, (((ca,), (cb,)), ((), ())), preferred_element_type=F32)


def near_first(i):
    a = i // 2
    return (a * (a + 1) // 2) % 4 + 4 * (i % 2)


def kernel(
    rate_ref, gain_ref, q_ref, k_ref, v_ref, g_ref,
    normed_ref, dq_ref, dk_ref, dv_ref,
    att, intra, go, dk_part, dv_part, total,
    ls, lr, ts, tr, cs, cr, rs_, rr, ins, inr,
    gs, gr, tsb, trb, csb, crb, rsb, rrb, lts, ltr,
    s_l, r_l, s_t, r_t, s_c, r_c, s_r, r_r, s_i, r_i,
    s_lb, r_lb, s_tb, r_tb, s_cb, r_cb, s_rb, r_rb, s_ib, r_ib,
):
    ctx = lax.axis_index("ctx")
    x = lax.axis_index("head")
    z, y, core = ctx // (NY * NCORE), (ctx // NCORE) % NY, ctx % NCORE
    r = core * NX + x
    size = q_ref.shape[1]

    def row_device(r2):
        return ((z * NY + y) * NCORE + r2 // NX, r2 % NX)

    def y_device(y2):
        return ((z * NY + y2) * NCORE + core, x)

    def z_device(z2):
        return ((z2 * NY + y) * NCORE + core, x)

    barrier = pltpu.get_barrier_semaphore()

    @pl.loop(1, ROW)
    def _(o):
        pl.semaphore_signal(barrier, inc=1, device_id=row_device((r + o) % ROW), device_id_type=MESH)

    @pl.loop(1, NY)
    def _(o):
        pl.semaphore_signal(barrier, inc=1, device_id=y_device((y + o) % NY), device_id_type=MESH)

    @pl.loop(1, NZ)
    def _(o):
        pl.semaphore_signal(barrier, inc=1, device_id=z_device((z + o) % NZ), device_id_type=MESH)

    pl.semaphore_wait(barrier, ROW + NY + NZ - 3)

    step_i = lax.broadcasted_iota(jnp.int32, (size, size), 0).astype(F32)
    step_j = lax.broadcasted_iota(jnp.int32, (size, size), 1).astype(F32)
    offset = step_i - step_j

    def mask(rate):
        return jnp.where(offset >= 0, jnp.exp(-rate * jnp.maximum(offset, 0.0)), 0.0)

    def head_decay(rate):
        return jnp.exp(-rate * (step_i + 1.0))

    def tail_decay(rate):
        return jnp.exp(-rate * (size - 1.0 - step_i))

    def span_decay(rate, stretches):
        return jnp.exp(jnp.full((1, size), -rate * (1.0 * size * stretches), F32))

    def row_copy(src, dst, s_sem, r_sem, o):
        r2 = (r + o) % ROW
        return pltpu.make_async_remote_copy(
            src_ref=src.at[r2], dst_ref=dst.at[r], send_sem=s_sem.at[o], recv_sem=r_sem.at[o],
            device_id=row_device(r2), device_id_type=MESH)

    def row_send(src, dst, s_sem, r_sem, o):
        @pl.when(o != 0)
        def _():
            row_copy(src, dst, s_sem, r_sem, o).start()

        @pl.when(o == 0)
        def _():
            pltpu.make_async_copy(src.at[r], dst.at[r], r_sem.at[0]).start()

    def row_arrived(src, dst, s_sem, r_sem, o):
        r2 = (r + ROW - o) % ROW

        @pl.when(o != 0)
        def _():
            pltpu.make_async_remote_copy(
                src_ref=src.at[r2], dst_ref=dst.at[r2], send_sem=s_sem.at[o], recv_sem=r_sem.at[o],
                device_id=row_device(r2), device_id_type=MESH).wait_recv()

        @pl.when(o == 0)
        def _():
            pltpu.make_async_copy(src.at[r], dst.at[r], r_sem.at[0]).wait()

    def y_copy(src, dst, s_sem, r_sem, o, sending):
        y2 = (y + o) % NY if sending else (y + NY - o) % NY
        return pltpu.make_async_remote_copy(
            src_ref=src.at[y2], dst_ref=dst.at[y if sending else y2],
            send_sem=s_sem.at[o], recv_sem=r_sem.at[o],
            device_id=y_device(y2), device_id_type=MESH)

    def z_copy(src, dst, s_sem, r_sem, o, to_later):
        z2 = z + o if to_later else z - o
        return pltpu.make_async_remote_copy(
            src_ref=src, dst_ref=dst.at[z], send_sem=s_sem.at[o], recv_sem=r_sem.at[o],
            device_id=z_device(z2), device_id_type=MESH)

    def z_arrival(src, dst, s_sem, r_sem, o, to_later):
        z2 = z - o if to_later else z + o
        return pltpu.make_async_remote_copy(
            src_ref=src, dst_ref=dst.at[z2], send_sem=s_sem.at[o], recv_sem=r_sem.at[o],
            device_id=z_device(z2), device_id_type=MESH)

    def z_inside(o, later):
        return z + o < NZ if later else z - o >= 0

    def carry(own, got, t_out, t_in, c_out, c_in, r_out, r_in, out, back,
              s_own, r_own, s_t2, r_t2, s_c2, r_c2, s_r2, r_r2, s_out, r_out2, forward):
        @pl.loop(0, ROW)
        def _(i):
            row_arrived(own, got, s_own, r_own, near_first(i))

        order = range(ROW) if forward else range(ROW - 1, -1, -1)

        @pl.loop(0, PER)
        def _(j):
            weight = span_decay(rate_ref[r * PER + j], 1)
            acc = None
            for c in order:
                piece = got[c, j].astype(F32)
                acc = piece if acc is None else acc * weight + piece
            t_out[j] = acc.astype(BF16)

        @pl.loop(1, NY)
        def _(o):
            y_copy(t_out, t_in, s_t2, r_t2, o, True).start()

        t_in[y] = t_out[y]

        @pl.loop(1, NY)
        def _(o):
            y_copy(t_out, t_in, s_t2, r_t2, o, False).wait_recv()

        rate = rate_ref[r * PER + y]
        weight = span_decay(rate, ROW)
        acc = None
        y_order = range(NY) if forward else range(NY - 1, -1, -1)
        for c in y_order:
            piece = t_in[c].astype(F32)
            acc = piece if acc is None else acc * weight + piece
        c_out[...] = acc.astype(BF16)

        @pl.loop(1, NZ)
        def _(o):
            @pl.when(z_inside(o, forward))
            def _():
                z_copy(c_out, c_in, s_c2, r_c2, o, forward).start()

        total[...] = jnp.zeros_like(total)
        column = span_decay(rate, ROW * NY)

        @pl.loop(0, NZ - 1)
        def _(i):
            o = NZ - 1 - i

            @pl.when(z_inside(o, not forward))
            def _():
                z_arrival(c_out, c_in, s_c2, r_c2, o, forward).wait_recv()
                z2 = z - o if forward else z + o
                total[...] = total[...] * column + c_in[z2].astype(F32)

        acc = total[...]
        for c in y_order:
            r_out[c] = acc.astype(BF16)
            acc = acc * weight + t_in[c].astype(F32)

        @pl.loop(1, NY)
        def _(o):
            y_copy(r_out, r_in, s_r2, r_r2, o, True).start()

        r_in[y] = r_out[y]

        @pl.loop(1, NY)
        def _(o):
            y_copy(r_out, r_in, s_r2, r_r2, o, False).wait_recv()

        @pl.loop(0, PER)
        def _(j):
            weight = span_decay(rate_ref[r * PER + j], 1)
            acc = r_in[j].astype(F32)
            for c in order:
                out[c, j] = acc.astype(BF16)
                acc = acc * weight + got[c, j].astype(F32)

        @pl.loop(0, ROW)
        def _(i):
            row_send(out, back, s_out, r_out2, near_first(ROW - 1 - i))

    @pl.loop(0, ROW)
    def _(i):
        o = near_first(ROW - 1 - i)
        r2 = (r + o) % ROW
        for j in range(PER):
            h = r2 * PER + j
            rate = rate_ref[h]
            key_decayed = (k_ref[h].astype(F32) * tail_decay(rate)).astype(BF16)
            ls[r2, j] = dot(key_decayed, v_ref[h], 0, 0).astype(BF16)
        row_send(ls, lr, s_l, r_l, o)

    @pl.loop(0, ROW)
    def _(i):
        for j in range(PER):
            h = i * PER + j
            scores = dot(q_ref[h], k_ref[h], 1, 1)
            weights = (scores * mask(rate_ref[h])).astype(BF16)
            att[h] = weights
            intra[h] = dot(weights, v_ref[h], 1, 0)

    carry(ls, lr, ts, tr, cs, cr, rs_, rr, ins, inr,
          s_l, r_l, s_t, r_t, s_c, r_c, s_r, r_r, s_i, r_i, True)

    @pl.loop(0, ROW)
    def _(i):
        o = near_first(i)
        row_arrived(ins, inr, s_i, r_i, o)
        r2 = (r + ROW - o) % ROW
        for j in range(PER):
            h = r2 * PER + j
            decay = head_decay(rate_ref[h])
            queries = q_ref[h]
            outputs = intra[h] + decay * dot(queries, inr[r2, j], 1, 0)
            inv_rms = lax.rsqrt(jnp.mean(outputs * outputs, axis=-1, keepdims=True) + 1e-06)
            unit = outputs * inv_rms
            gain = gain_ref[h]
            normed_ref[h] = (unit * gain).astype(BF16)
            scaled = gain * g_ref[h].astype(F32)
            grad_out = (
                inv_rms * (scaled - unit * jnp.mean(scaled * unit, axis=-1, keepdims=True))
            ).astype(BF16)
            go[h] = grad_out
            query_decayed = (queries.astype(F32) * decay).astype(BF16)
            gs[r2, j] = dot(query_decayed, grad_out, 0, 0).astype(BF16)
        row_send(gs, gr, s_lb, r_lb, (ROW - o) % ROW)

    @pl.loop(0, ROW)
    def _(i):
        for j in range(PER):
            h = i * PER + j
            rate = rate_ref[h]
            grad_out = go[h]
            queries = q_ref[h]
            score_grad = (dot(grad_out, v_ref[h], 1, 1) * mask(rate)).astype(BF16)
            dq = dot(score_grad, k_ref[h], 1, 0)
            dq = dq + head_decay(rate) * dot(grad_out, inr[i, j], 1, 1)
            dq_ref[h] = dq.astype(BF16)
            dk_part[h] = dot(score_grad, queries, 0, 0)
            dv_part[h] = dot(att[h], grad_out, 0, 0)

    carry(gs, gr, tsb, trb, csb, crb, rsb, rrb, lts, ltr,
          s_lb, r_lb, s_tb, r_tb, s_cb, r_cb, s_rb, r_rb, s_ib, r_ib, False)

    @pl.loop(0, ROW)
    def _(i):
        o = near_first(i)
        row_arrived(lts, ltr, s_ib, r_ib, o)
        r2 = (r + ROW - o) % ROW
        for j in range(PER):
            h = r2 * PER + j
            decay = tail_decay(rate_ref[h])
            later = ltr[r2, j]
            dk_ref[h] = (dk_part[h] + decay * dot(v_ref[h], later, 1, 1)).astype(BF16)
            dv_ref[h] = (dv_part[h] + decay * dot(k_ref[h], later, 1, 0)).astype(BF16)

    @pl.loop(1, ROW)
    def _(o):
        row_copy(ls, lr, s_l, r_l, o).wait_send()
        row_copy(ins, inr, s_i, r_i, o).wait_send()
        row_copy(gs, gr, s_lb, r_lb, o).wait_send()
        row_copy(lts, ltr, s_ib, r_ib, o).wait_send()

    @pl.loop(1, NY)
    def _(o):
        y_copy(ts, tr, s_t, r_t, o, True).wait_send()
        y_copy(rs_, rr, s_r, r_r, o, True).wait_send()
        y_copy(tsb, trb, s_tb, r_tb, o, True).wait_send()
        y_copy(rsb, rrb, s_rb, r_rb, o, True).wait_send()

    @pl.loop(1, NZ)
    def _(o):
        @pl.when(z_inside(o, True))
        def _():
            z_copy(cs, cr, s_c, r_c, o, True).wait_send()

        @pl.when(z_inside(o, False))
        def _():
            z_copy(csb, crb, s_cb, r_cb, o, False).wait_send()


def local(queries, key_vectors, value_vectors, output_grad, decay_rate, norm_gain):
    length, heads, size = queries.shape
    by_head = [jnp.transpose(a, (1, 0, 2)) for a in (queries, key_vectors, value_vectors, output_grad)]
    tile = (size, size)
    whole = pl.BlockSpec(memory_space=pltpu.VMEM)
    one_way = [
        pltpu.VMEM((ROW, PER) + tile, BF16),
        pltpu.VMEM((ROW, PER) + tile, BF16),
        pltpu.VMEM((NY,) + tile, BF16),
        pltpu.VMEM((NY,) + tile, BF16),
        pltpu.VMEM(tile, BF16),
        pltpu.VMEM((NZ,) + tile, BF16),
        pltpu.VMEM((NY,) + tile, BF16),
        pltpu.VMEM((NY,) + tile, BF16),
        pltpu.VMEM((ROW, PER) + tile, BF16),
        pltpu.VMEM((ROW, PER) + tile, BF16),
    ]
    sems = [pltpu.SemaphoreType.DMA((n,)) for n in (ROW, ROW, NY, NY, NZ, NZ, NY, NY, ROW, ROW)]
    results = pl.pallas_call(
        kernel,
        out_shape=[jax.ShapeDtypeStruct((heads, length, size), BF16)] * 4,
        in_specs=[pl.BlockSpec(memory_space=pltpu.SMEM)] + [whole] * 5,
        out_specs=[whole] * 4,
        scratch_shapes=[
            pltpu.VMEM((heads,) + tile, BF16),
            pltpu.VMEM((heads,) + tile, F32),
            pltpu.VMEM((heads,) + tile, BF16),
            pltpu.VMEM((heads,) + tile, F32),
            pltpu.VMEM((heads,) + tile, F32),
            pltpu.VMEM(tile, F32),
        ] + one_way + one_way + sems + sems,
        compiler_params=pltpu.CompilerParams(
            collective_id=0, has_side_effects=True, vmem_limit_bytes=60 * 1024 * 1024
        ),
    )(decay_rate, norm_gain.reshape(heads, 1, size), *by_head)
    return tuple(jnp.transpose(a, (1, 0, 2)) for a in results)


def solution(mesh):
    spec = P(("ctx", "head"), None, None)
    return jax.shard_map(
        local, mesh=mesh, in_specs=(spec,) * 4 + (P(), P()), out_specs=(spec,) * 4, check_vma=False
    )
```

```python
import jax
import jax.numpy as jnp
from jax import lax
from jax.experimental import pallas as pl
from jax.experimental.pallas import tpu as pltpu
from jax.sharding import PartitionSpec as P

MESH = pl.DeviceIdType.MESH
NZ, NY, NCORE, NX = 8, 4, 2, 4
ROW = NCORE * NX
PLANE = NY * ROW
GROUPS = 4
NEAR_ROW = (0, 4, 1, 5, 3, 7, 2, 6)
NEAR_Y = (0, 1, 3, 2)
LATER = (("states", 0), ("inside", 2), ("fold", 3), ("inc", 5), ("out", 7), ("grads", 9), ("fold_back", 10),
         ("inc_back", 12), ("fin", 14))
F32 = jnp.float32
BF16 = jnp.bfloat16


def dot(a, b, ca, cb):
    return lax.dot_general(a, b, (((ca,), (cb,)), ((), ())), preferred_element_type=F32)


def kernel(
    rate_ref, gain_ref, q_hbm, k_hbm, v_hbm, g_hbm,
    normed_hbm, dq_hbm, dk_hbm, dv_hbm,
    tok, q_ref, k_ref, v_ref, g_ref, normed_ref, dq_ref, dk_ref, dv_ref,
    masks, heads_decay, tails_decay, att, intra, go, dk_part, dv_part,
    ls, lr, ins, inr, gs, gr, lts, ltr, cs, cr, csb, crb,
    s_row, r_row, s_z, r_z, in_sem, out_sem,
):
    ctx = lax.axis_index("ctx")
    x = lax.axis_index("head")
    z, y, core = ctx // (NY * NCORE), (ctx // NCORE) % NY, ctx % NCORE
    row = core * NX + x
    me = y * ROW + row
    heads, size = q_ref.shape[0], q_ref.shape[1]
    per = heads // GROUPS
    cut = PLANE // per
    depth = size // cut

    loads = [pltpu.make_async_copy(a, tok.at[n], in_sem.at[n]) for n, a in enumerate((k_hbm, v_hbm, q_hbm, g_hbm))]
    for load in loads:
        load.start()

    ys = [(y + d) % NY for d in range(NY)]
    rows = [(row + d) % ROW for d in range(ROW)]
    cores = [a // NX for a in rows]
    xs = [a % NX for a in rows]

    def plane_device(dy, dr):
        return ((z * NY + ys[dy]) * NCORE + cores[dr], xs[dr])

    def z_device(z2):
        return ((z2 * NY + y) * NCORE + core, x)

    cr[...] = jnp.zeros_like(cr)
    crb[...] = jnp.zeros_like(crb)

    others = [(dy, dr) for dy in reversed(NEAR_Y) for dr in reversed(NEAR_ROW) if dy or dr]
    barrier = pltpu.get_barrier_semaphore()
    for dy, dr in others:
        pl.semaphore_signal(barrier, inc=1, device_id=plane_device(dy, dr), device_id_type=MESH)
    for d in range(1, NZ):
        pl.semaphore_signal(barrier, inc=1, device_id=z_device((z + d) % NZ), device_id_type=MESH)

    half = heads // 2
    for n, ref in enumerate((k_ref, v_ref, q_ref, g_ref)):
        loads[n].wait()
        for hh in range(2):
            @pl.loop(0, size // 16)
            def _(t):
                ref[pl.ds(hh * half, half), pl.ds(t * 16, 16), :] = jnp.transpose(
                    tok[n, pl.ds(t * 16, 16), pl.ds(hh * half, half), :], (1, 0, 2))

    pl.semaphore_wait(barrier, PLANE + NZ - 2)

    step_i = lax.broadcasted_iota(jnp.int32, (size, size), 0).astype(F32)
    step_j = lax.broadcasted_iota(jnp.int32, (size, size), 1).astype(F32)

    def span_decay(rate, stretches):
        return jnp.exp(jnp.full((1, size), -rate * (1.0 * size * stretches), F32))

    def plane_copy(src, dst, phase, g, dy, dr):
        return pltpu.make_async_remote_copy(
            src_ref=src.at[g, ys[dy] * ROW + rows[dr]], dst_ref=dst.at[g, me],
            send_sem=s_row.at[phase, g], recv_sem=r_row.at[phase, g],
            device_id=plane_device(dy, dr), device_id_type=MESH)

    def plane_all(src, dst, phase, g):
        return pltpu.make_async_remote_copy(
            src_ref=src.at[g, pl.ds(0, PLANE - 1)], dst_ref=dst.at[g, pl.ds(0, PLANE - 1)],
            send_sem=s_row.at[phase, g], recv_sem=r_row.at[phase, g],
            device_id=plane_device(0, 1), device_id_type=MESH)

    def send(src, dst, phase, g):
        for dy, dr in others:
            plane_copy(src, dst, phase, g, dy, dr).start()
        dst[g, me] = src[g, me]

    def z_copy(src, dst, way, g, d, sending):
        towards = d if way == 0 else -d
        z2 = z + towards if sending else z - towards
        slot = z if sending else z2
        there = jnp.logical_and(z2 >= 0, z2 < NZ)
        return there, pltpu.make_async_remote_copy(
            src_ref=src.at[g], dst_ref=dst.at[g, slot],
            send_sem=s_z.at[way, g, d], recv_sem=r_z.at[way, g, d],
            device_id=z_device(z2), device_id_type=MESH)

    def fold(own, got, c_out, c_in, phase, way, g):
        plane_all(own, got, phase, g).wait_recv()
        weight = span_decay(rate_ref[g * per + me // cut], 1)
        order = range(PLANE) if way == 0 else range(PLANE - 1, -1, -1)
        acc = None
        for c in order:
            piece = got[g, c].astype(F32)
            acc = piece if acc is None else acc * weight + piece
        c_out[g] = acc.astype(BF16)
        for d in range(1, NZ):
            there, copy = z_copy(c_out, c_in, way, g, d, True)

            @pl.when(there)
            def _():
                copy.start()

    def inc(own, got, c_out, c_in, out, back, phase, way, g):
        for d in range(1, NZ):
            there, copy = z_copy(c_out, c_in, way, g, d, False)

            @pl.when(there)
            def _():
                copy.wait_recv()

        rate = rate_ref[g * per + me // cut]
        weight = span_decay(rate, 1)
        plane = span_decay(rate, PLANE)
        acc = jnp.zeros((depth, size), F32)
        for d in range(NZ - 1, 0, -1):
            z2 = (z + NZ - d) % NZ if way == 0 else (z + d) % NZ
            acc = acc * plane + c_in[g, z2].astype(F32)
        order = range(PLANE) if way == 0 else range(PLANE - 1, -1, -1)
        for c in order:
            out[g, c] = acc.astype(BF16)
            acc = acc * weight + got[g, c].astype(F32)
        send(out, back, phase, g)

    def each_head(g, body):
        @pl.loop(0, per // 4)
        def _(i):
            for j in range(4):
                body(g * per + i * 4 + j, i * 4 + j)

    def put(dst, g, n, state):
        dst[g, pl.ds(n * cut, cut)] = state.astype(BF16).reshape(cut, depth, size)

    def take(src, g, n):
        return src[g, pl.ds(n * cut, cut)].reshape(size, size)

    def results_copy(n, hbm, hh):
        part = pl.ds(hh * half, half)
        return pltpu.make_async_copy(tok.at[n, :, part], hbm.at[:, part], out_sem.at[n, hh])

    def results_out(n, ref, hbm, g):
        @pl.when((g + 1) * per % half == 0)
        def _():
            hh = g * per // half

            @pl.loop(0, size // 16)
            def _(t):
                tok[n, pl.ds(t * 16, 16), pl.ds(hh * half, half), :] = jnp.transpose(
                    ref[pl.ds(hh * half, half), pl.ds(t * 16, 16), :], (1, 0, 2))
            results_copy(n, hbm, hh).start()

    def states(g):
        def body(h, n):
            tail = jnp.exp(-rate_ref[h] * (size - 1.0 - step_i))
            tails_decay[h] = tail
            key_decayed = (k_ref[h].astype(F32) * tail).astype(BF16)
            put(ls, g, n, dot(key_decayed, v_ref[h], 0, 0))
        each_head(g, body)
        send(ls, lr, 0, g)

    def inside(g):
        def body(h, n):
            offset = step_i - step_j
            mask = jnp.where(offset >= 0, jnp.exp(-rate_ref[h] * jnp.maximum(offset, 0.0)), 0.0)
            masks[h] = mask
            weights = (dot(q_ref[h], k_ref[h], 1, 1) * mask).astype(BF16)
            att[h] = weights
            intra[h] = dot(weights, v_ref[h], 1, 0)
        each_head(g, body)

    def out(g):
        plane_all(ins, inr, 1, g).wait_recv()

        def body(h, n):
            decay = jnp.exp(-rate_ref[h] * (step_i + 1.0))
            heads_decay[h] = decay
            queries = q_ref[h]
            outputs = intra[h] + decay * dot(queries, take(inr, g, n), 1, 0)
            inv_rms = lax.rsqrt(jnp.mean(outputs * outputs, axis=-1, keepdims=True) + 1e-06)
            unit = outputs * inv_rms
            gain = gain_ref[h]
            normed_ref[h] = (unit * gain).astype(BF16)
            scaled = gain * g_ref[h].astype(F32)
            grad_out = (
                inv_rms * (scaled - unit * jnp.mean(scaled * unit, axis=-1, keepdims=True))
            ).astype(BF16)
            go[h] = grad_out
            query_decayed = (queries.astype(F32) * decay).astype(BF16)
            put(gs, g, n, dot(query_decayed, grad_out, 0, 0))
        each_head(g, body)
        send(gs, gr, 2, g)
        results_out(0, normed_ref, normed_hbm, g)

    def grads(g):
        def body(h, n):
            grad_out = go[h]
            score_grad = (dot(grad_out, v_ref[h], 1, 1) * masks[h]).astype(BF16)
            dq = dot(score_grad, k_ref[h], 1, 0)
            dq = dq + heads_decay[h] * dot(grad_out, take(inr, g, n), 1, 1)
            dq_ref[h] = dq.astype(BF16)
            dk_part[h] = dot(score_grad, q_ref[h], 0, 0)
            dv_part[h] = dot(att[h], grad_out, 0, 0)
        each_head(g, body)
        results_out(1, dq_ref, dq_hbm, g)

    def fin(g):
        plane_all(lts, ltr, 3, g).wait_recv()

        def body(h, n):
            decay = tails_decay[h]
            later = take(ltr, g, n)
            dk_ref[h] = (dk_part[h] + decay * dot(v_ref[h], later, 1, 1)).astype(BF16)
            dv_ref[h] = (dv_part[h] + decay * dot(k_ref[h], later, 1, 0)).astype(BF16)
        each_head(g, body)
        results_out(2, dk_ref, dk_hbm, g)
        results_out(3, dv_ref, dv_hbm, g)

    stages = {
        "states": states,
        "inside": inside,
        "fold": lambda g: fold(ls, lr, cs, cr, 0, 0, g),
        "inc": lambda g: inc(ls, lr, cs, cr, ins, inr, 1, 0, g),
        "out": out,
        "grads": grads,
        "fold_back": lambda g: fold(gs, gr, csb, crb, 2, 1, g),
        "inc_back": lambda g: inc(gs, gr, csb, crb, lts, ltr, 3, 1, g),
        "fin": fin,
    }

    @pl.loop(0, GROUPS + max(late for _, late in LATER))
    def _(s):
        for name, late in LATER:
            @pl.when(jnp.logical_and(s >= late, s < late + GROUPS))
            def _():
                stages[name](s - late)

    @pl.loop(0, GROUPS)
    def _(g):
        for phase, (src, dst) in enumerate(((ls, lr), (ins, inr), (gs, gr), (lts, ltr))):
            plane_all(src, dst, phase, g).wait_send()
        for way, (src, dst) in enumerate(((cs, cr), (csb, crb))):
            for d in range(1, NZ):
                there, copy = z_copy(src, dst, way, g, d, True)

                @pl.when(there)
                def _():
                    copy.wait_send()

    for n, hbm in enumerate((normed_hbm, dq_hbm, dk_hbm, dv_hbm)):
        for hh in range(2):
            results_copy(n, hbm, hh).wait()


def hand_on(*refs):
    results, outs, (held, in_sem, out_sem) = refs[:4], refs[4:8], refs[8:]
    chunks = in_sem.shape[1]
    rows = held.shape[1] // chunks
    parts = [(n, c, pl.ds(c * rows, rows)) for c in range(chunks) for n in range(4)]
    loads = [pltpu.make_async_copy(results[n].at[part], held.at[n, part], in_sem.at[n, c]) for n, c, part in parts]
    stores = [pltpu.make_async_copy(held.at[n, part], outs[n].at[part], out_sem.at[n, c]) for n, c, part in parts]
    for load in loads:
        load.start()
    for load, store in zip(loads, stores):
        load.wait()
        store.start()
    for store in stores:
        store.wait()


def local(queries, key_vectors, value_vectors, output_grad, decay_rate, norm_gain):
    length, heads, size = queries.shape
    tile = (size, size)
    every = lambda dtype: pltpu.VMEM((heads,) + tile, dtype)
    depth = size * heads // GROUPS // PLANE
    pieces = pltpu.VMEM((GROUPS, PLANE, depth, size), BF16)
    columns = [pltpu.VMEM((GROUPS, depth, size), BF16), pltpu.VMEM((GROUPS, NZ, depth, size), BF16)]
    by_token = jax.ShapeDtypeStruct((length, heads, size), BF16)
    results = pl.pallas_call(
        kernel,
        out_shape=[by_token] * 4,
        in_specs=[pl.BlockSpec(memory_space=pltpu.SMEM), pl.BlockSpec(memory_space=pltpu.VMEM)]
        + [pl.BlockSpec(memory_space=pl.ANY)] * 4,
        out_specs=[pl.BlockSpec(memory_space=pl.ANY)] * 4,
        scratch_shapes=[pltpu.VMEM((4, length, heads, size), BF16)]
        + [every(BF16)] * 8
        + [every(F32)] * 3
        + [every(BF16), every(F32), every(BF16), every(F32), every(F32)]
        + [pieces] * 8
        + columns + columns
        + [
            pltpu.SemaphoreType.DMA((4, GROUPS)),
            pltpu.SemaphoreType.DMA((4, GROUPS)),
            pltpu.SemaphoreType.DMA((2, GROUPS, NZ)),
            pltpu.SemaphoreType.DMA((2, GROUPS, NZ)),
            pltpu.SemaphoreType.DMA((4,)),
            pltpu.SemaphoreType.DMA((4, 2)),
        ],
        compiler_params=pltpu.CompilerParams(
            collective_id=0, has_side_effects=True, vmem_limit_bytes=60 * 1024 * 1024
        ),
    )(decay_rate, norm_gain.reshape(heads, 1, size), queries, key_vectors, value_vectors, output_grad)
    return tuple(pl.pallas_call(
        hand_on,
        out_shape=[by_token] * 4,
        in_specs=[pl.BlockSpec(memory_space=pl.ANY)] * 4,
        out_specs=[pl.BlockSpec(memory_space=pl.ANY)] * 4,
        scratch_shapes=[
            pltpu.VMEM((4, length, heads, size), BF16),
            pltpu.SemaphoreType.DMA((4, 4)),
            pltpu.SemaphoreType.DMA((4, 4)),
        ],
        compiler_params=pltpu.CompilerParams(vmem_limit_bytes=60 * 1024 * 1024),
    )(*results))


def solution(mesh):
    spec = P(("ctx", "head"), None, None)
    return jax.shard_map(
        local, mesh=mesh, in_specs=(spec,) * 4 + (P(), P()), out_specs=(spec,) * 4, check_vma=False
    )
```
